32 devices in a mesh: hour: 2 (over y), pair: 4 (over z), freq: 2 (over x), sub: 2 (over core).
Axes of the slice: x: 2, y: 2, z: 4, core: 2. Of those that a mesh axis runs over, the one named last changes fastest.
Arguments:
- raw: float32 [512, 4096], P('freq', ('hour', 'pair', 'sub')), parts along dimension 1, may hold values from -60 to 60
- offsets: int32 [16], P(('hour', 'pair', 'sub')), parts along dimension 0, may hold values from 0 to 255
- pair_mask: int32 [4, 2], P('pair'), may hold values 0 or 1
Outputs:
- correlations: bfloat16 [8, 3, 128, 128, 256], P(('hour', 'pair'), None, 'sub', 'freq'), parts along dimension 0
The draws below stay inside these ranges and needn't reach their ends.
There are 2 independent parts, one for each index of `hour`. The reference program is written for one: setup_inputs(seed, part) draws one part's arguments, and reference() takes and returns one part's arrays. A program takes and returns all parts, laid end to end along the dimension named above; an argument that names none is the same for every part. Nothing has to cross between parts.
All inputs are finite; a program needn't handle non-finite values. No bound on the sum of `pair_mask` on one device may be relied on, other than what follows from the above.
Results may differ from the reference program's by a relative error of at most 0.0056.
Values may be sent and summed in bfloat16 or wider, within the bound.
No kernel may reach another device: no remote copies, remote signals or barrier semaphores. Data moves between devices by JAX's collectives and lax.ppermute only.
A program may use at most 64 MiB of HBM per device.

```python
import math
import jax
import jax.numpy as jnp
from jax import lax

CH = 128
F = 256
REACH = 2
LAGS = 256
NBLK = 4
STEP = 256
W = 8


def draw_raw(key, part):
    first, second, third = jax.random.split(key, 3)
    total = W * STEP
    common = jax.random.normal(second, (total,), jnp.float32)
    gains = jax.random.uniform(third, (CH * NBLK, 1), jnp.float32, 0.3, 1.0)
    noise = jax.random.normal(first, (CH * NBLK, total), jnp.float32)
    return jnp.clip(noise + gains * common[None, :], -60.0, 60.0)


def with_ends(values, own_key, least, high):
    index_at = [jax.random.randint(jax.random.fold_in(own_key, axis), (), 0, length) for axis, length in enumerate(values.shape)]
    widest = values.shape.index(max(values.shape))
    next_to = index_at[:widest] + [(index_at[widest] + 1) % values.shape[widest]] + index_at[widest + 1:]
    return values.at[tuple(index_at)].set(least).at[tuple(next_to)].set(high)


def setup_inputs(seed: int = 0, part: int = 0) -> dict:
    streams_of = jax.random.split(jax.random.key(seed), 4)
    own_keys = jax.random.split(jax.random.fold_in(streams_of[3], part), 4)
    raw = draw_raw(jax.random.fold_in(jax.random.fold_in(streams_of[3], part), 71), part)
    offsets = with_ends(jax.random.randint(own_keys[1], (W,), 0, F), jax.random.fold_in(own_keys[1], 1), 0, F - 1).astype(jnp.int32)
    pair_mask = with_ends((jax.random.randint(streams_of[2], (NBLK, REACH), 0, 2) < 1).astype(jnp.int32), jax.random.fold_in(streams_of[2], 1), 0, 1)
    return dict(raw=raw, offsets=offsets, pair_mask=pair_mask)


def dft_basis(freqs, imaginary, span):
    samples = jnp.arange(span, dtype=jnp.int32)
    phase = samples[:, None] * freqs[None, :] % span
    angle = 2.0 * math.pi / span * phase.astype(jnp.float32)
    values = jnp.where(imaginary[None, :], -jnp.sin(angle), jnp.cos(angle)) / math.sqrt(span)
    return values.astype(jnp.bfloat16)

def lag_basis(freqs, imaginary, span, lag_count, bins):
    delays = jnp.arange(lag_count, dtype=jnp.int32) - lag_count // 2
    phase = freqs[:, None] * delays[None, :] % span
    angle = 2.0 * math.pi / span * phase.astype(jnp.float32)
    values = jnp.where(imaginary[:, None], -jnp.sin(angle), jnp.cos(angle)) / math.sqrt(bins)
    return values.astype(jnp.bfloat16)

def tapered(windows):
    span = windows.shape[-1]
    centred = windows - lax.optimization_barrier(jnp.mean(windows, axis=-1, keepdims=True))
    power = lax.optimization_barrier(jnp.mean(centred * centred, axis=-1, keepdims=True))
    ticks = jnp.arange(span, dtype=jnp.float32)
    hann_taper = 0.5 - 0.5 * jnp.cos(2.0 * math.pi / span * ticks)
    return (centred * lax.rsqrt(power + 1e-05) * hann_taper).astype(jnp.bfloat16)

def cross_spectra(first_block, second_block, factor):
    row_count, count, width = first_block.shape
    bins = width // 2
    left = first_block.reshape(row_count, count, 2, bins).astype(jnp.float32)
    right = second_block.reshape(second_block.shape[0], count, 2, bins).astype(jnp.float32)
    turned = jnp.stack([left[:, :, 1], -left[:, :, 0]], axis=2)
    real_part = jnp.einsum('rwtf,cwtf->rcf', left, right)
    imaginary_part = jnp.einsum('rwtf,cwtf->rcf', turned, right)
    return jnp.concatenate([real_part, imaginary_part], axis=-1) * factor

def reference(raw, offsets, pair_mask):
    span = 2 * F
    padded = jnp.concatenate([raw, jnp.zeros((raw.shape[0], span), jnp.float32)], axis=1)
    starts = (jnp.arange(W, dtype=jnp.int32) * STEP + offsets).astype(jnp.int32)
    column = jnp.arange(span, dtype=jnp.int32)
    freqs = (column % F).astype(jnp.int32)
    imaginary = column >= F
    basis = dft_basis(freqs, imaginary, span)

    def block_spectra(index):
        channels = lax.dynamic_slice_in_dim(padded, (index * CH).astype(jnp.int32), CH, 0)
        windows = jax.vmap(lambda begin: lax.dynamic_slice_in_dim(channels, begin, span, 1), out_axes=1)(starts)
        return jnp.dot(tapered(windows), basis, preferred_element_type=jnp.float32).astype(jnp.bfloat16)
    spectra = lax.map(block_spectra, jnp.arange(NBLK, dtype=jnp.int32))
    lag_table = lag_basis(freqs, imaginary, span, LAGS, F)

    def block_pairs(index):
        mine = spectra[index]
        results = []
        for offset in range(REACH + 1):
            other = index + offset
            partner = spectra[jnp.minimum(other, NBLK - 1)]
            keep = other < NBLK
            if offset > 0:
                keep = keep & (pair_mask[index, offset - 1] == 1)
            term = cross_spectra(mine, partner, 1.0 / W)
            term = jnp.where(keep, term, 0.0).astype(jnp.bfloat16)
            results.append(jnp.dot(term, lag_table, preferred_element_type=jnp.float32).astype(jnp.bfloat16))
        return jnp.stack(results)
    return lax.map(block_pairs, jnp.arange(NBLK, dtype=jnp.int32))
```

```python
import functools
import math

import jax
import jax.numpy as jnp
import numpy as np
from jax import lax
from jax.experimental import pallas as pl
from jax.experimental.pallas import tpu as pltpu
from jax.sharding import PartitionSpec as P

F = 256
REACH = 2
LAGS = 256
STEP = 256
LANES = 128
PACK = 16
EXTRA = 8
ROWS_PER_STEP = 16


def rotated(value, axis, steps):
    count = lax.axis_size(axis)
    return lax.ppermute(value, axis, [(source, (source + steps) % count) for source in range(count)])


def tables(span, windows):
    samples = np.arange(span)
    freqs = np.arange(F)
    angle = 2.0 * math.pi / span * (samples[:, None] * freqs[None, :] % span)
    basis = np.concatenate([np.cos(angle), -np.sin(angle)], axis=1) / math.sqrt(span)
    delays = np.arange(LAGS) - LAGS // 2
    angle = 2.0 * math.pi / span * (freqs[:, None] * delays[None, :] % span)
    lag = np.concatenate([np.cos(angle), -np.sin(angle)], axis=0) / math.sqrt(F)
    taper = 0.5 - 0.5 * np.cos(2.0 * math.pi / span * samples)
    return (
        jnp.asarray(basis.T.astype(np.float32), jnp.bfloat16),
        jnp.asarray((lag / windows).astype(np.float32), jnp.bfloat16),
        jnp.asarray(np.broadcast_to(taper[:, None], (span, LANES)), jnp.float32),
    )


def pack_kernel(dims, raw_ref, keep_ref, *send_refs):
    freq_count, blocks, chans, width, parts, tp = dims
    mine = lax.axis_index("freq")
    for shift, out in enumerate((keep_ref, *send_refs)):
        part = lax.rem(mine + shift, freq_count)
        for block in range(blocks):
            start = pl.multiple_of(block * chans + part * width, width)
            rows = raw_ref[pl.ds(start, width), :]
            stacked = jnp.concatenate([rows[:, i * tp : (i + 1) * tp] for i in range(parts)], axis=0)
            out[block] = stacked.T


def route_kernel(dims, offset_ref, *refs):
    pair_count, freq_count, blocks, tp, local = dims
    ins, rest = refs[:freq_count], refs[freq_count:]
    near, far, held = rest[:pair_count], rest[pair_count : 2 * pair_count], rest[-1]
    mine = lax.axis_index("freq")
    here = lax.axis_index("pair")
    for shift, source in enumerate(ins):
        owner = lax.rem(mine + freq_count - shift, freq_count)
        for block in range(blocks):
            held[owner * blocks + block] = source[block]
    lane = lax.broadcasted_iota(jnp.int32, (EXTRA, LANES), 1)
    note = jnp.zeros((EXTRA, LANES), jnp.float32)
    for i in range(local):
        note = jnp.where(lane == i, offset_ref[i].astype(jnp.float32), note)
    for shift in range(pair_count):
        near[shift][0:tp, :] = held[lax.rem(here + shift, pair_count)]
        near[shift][tp : tp + EXTRA, :] = note
        for ahead in range(1, REACH + 1):
            far[shift][ahead - 1] = held[lax.rem(here + shift + ahead, pair_count)]


def correlate_kernel(dims, mask_ref, *refs):
    (pair_count, freq_count, sub_count, local, seg, width, parts, tp, row_parts, windows, span) = dims
    near_count = freq_count * sub_count
    far_count = pair_count * sub_count
    near = refs[:near_count]
    far = refs[near_count : near_count + far_count]
    basis_ref, lag_ref, taper_ref, out_ref, starts, x_ref, spec_ref, row_ref, cross_ref = refs[
        near_count + far_count :
    ]
    total = windows * STEP
    cols = (REACH + 1) * width
    row_count = row_parts * width
    depth = 2 * windows * PACK
    wide = cross_ref.shape[2]
    step = pl.program_id(0)
    here = lax.axis_index("pair")
    mine = lax.axis_index("freq")
    core = lax.axis_index("sub")

    def place(slot, segment, piece):
        tile, lo = divmod(slot * width, LANES)
        for i in range(parts):
            base = pl.multiple_of(segment * seg + i * tp, tp)
            x_ref[tile, pl.ds(base, tp), lo : lo + width] = piece[:, i * width : (i + 1) * width]

    @pl.when(step == 0)
    def _():
        x_ref[:, total : total + span, :] = jnp.zeros((x_ref.shape[0], span, LANES), jnp.float32)
        if cols + row_count < x_ref.shape[0] * LANES:
            x_ref[x_ref.shape[0] - 1] = jnp.zeros(x_ref.shape[1:], jnp.float32)
        for turn in range(sub_count):
            source_core = lax.rem(core + sub_count - turn, sub_count)
            for shift in range(pair_count):
                source = lax.rem(here + pair_count - shift, pair_count)
                segment = source * sub_count + source_core
                piece = near[turn * freq_count]
                place(0, segment, piece[shift, 0:tp, :])
                note = piece[shift, tp : tp + EXTRA, :]
                for i in range(local):
                    number = jnp.max(note[:, i : i + 1]).astype(jnp.int32)
                    window = segment * local + i
                    starts[window] = window * STEP + number
                for ahead in range(REACH):
                    place(1 + ahead, segment, far[turn * pair_count + shift][ahead])
                for i in range(row_parts):
                    part = core * row_parts + i
                    for k in range(freq_count):

                        @pl.when(lax.rem(mine + freq_count - part, freq_count) == k)
                        def _(k=k, i=i, segment=segment, shift=shift, turn=turn):
                            place(REACH + 1 + i, segment, near[turn * freq_count + k][shift, 0:tp, :])

        def spectra(window, unused):
            tapered = []
            for tile in range(x_ref.shape[0]):
                values = x_ref[tile, pl.ds(starts[window], span), :]
                centred = values - jnp.mean(values, axis=0, keepdims=True)
                power = jnp.mean(centred * centred, axis=0, keepdims=True)
                tapered.append((centred * lax.rsqrt(power + 1e-05) * taper_ref[...]).astype(jnp.bfloat16))
            spec_ref[window] = jnp.dot(
                basis_ref[...], jnp.concatenate(tapered, axis=1), preferred_element_type=jnp.float32
            ).astype(jnp.bfloat16)
            return unused

        lax.fori_loop(0, windows, spectra, 0)
        lane = lax.broadcasted_iota(jnp.int32, (PACK, depth), 1)
        diagonal = lax.rem(lane, PACK) == lax.broadcasted_iota(jnp.int32, (PACK, depth), 0)
        lo = cols // LANES * LANES
        hi = -(-(cols + row_count) // LANES) * LANES

        def group(index, unused):
            real = pl.multiple_of(index * PACK, PACK)
            imag = pl.multiple_of(F + index * PACK, PACK)
            same, turned = [], []
            for window in range(windows):
                first = spec_ref[window, pl.ds(real, PACK), :]
                second = spec_ref[window, pl.ds(imag, PACK), :]
                same += [first, second]
                turned += [-second, first]
            same = jnp.concatenate(same, axis=0)
            turned = jnp.concatenate(turned, axis=0)
            right = jnp.concatenate([same[:, :wide], turned[:, :wide]], axis=1)
            row_ref[...] = same[:, lo:hi].astype(jnp.float32).T[cols - lo : cols - lo + row_count]
            left = jnp.concatenate(
                [
                    jnp.where(diagonal, jnp.broadcast_to(row_ref[r : r + 1, :], (PACK, depth)), 0.0).astype(
                        jnp.bfloat16
                    )
                    for r in range(row_count)
                ],
                axis=0,
            )
            term = jnp.dot(left, right, preferred_element_type=jnp.float32).astype(jnp.bfloat16)
            term = term.reshape(row_count, PACK, 2 * wide)
            cross_ref[:, pl.ds(real, PACK), :] = term[:, :, :wide]
            cross_ref[:, pl.ds(imag, PACK), :] = term[:, :, wide:]
            return unused

        lax.fori_loop(0, F // PACK, group, 0)

    keeps = [None] + [
        (here + ahead < pair_count) & (mask_ref[0, ahead - 1] == 1) for ahead in range(1, REACH + 1)
    ]
    for r in range(out_ref.shape[2]):
        result = lax.dot_general(
            cross_ref[step * out_ref.shape[2] + r],
            lag_ref[...],
            (((0,), (0,)), ((), ())),
            preferred_element_type=jnp.float32,
        )
        for ahead, keep in enumerate(keeps):
            value = result[ahead * width : (ahead + 1) * width]
            if keep is not None:
                value = jnp.where(keep, value, 0.0)
            out_ref[0, ahead, r] = value.astype(jnp.bfloat16)


def body(raw, offsets, pair_mask):
    pair_count = lax.axis_size("pair")
    freq_count = lax.axis_size("freq")
    sub_count = lax.axis_size("sub")
    local = offsets.shape[0]
    seg = raw.shape[1]
    span = 2 * F
    chans = raw.shape[0] * freq_count // pair_count
    blocks = pair_count // freq_count
    width = chans // freq_count
    row_count = chans // sub_count
    row_parts = row_count // width
    parts = LANES // width
    tp = seg // parts
    windows = pair_count * sub_count * local
    vmem = pl.BlockSpec(memory_space=pltpu.VMEM)
    smem = pl.BlockSpec(memory_space=pltpu.SMEM)
    unit = jax.ShapeDtypeStruct((blocks, tp, LANES), jnp.float32)
    packed = pl.pallas_call(
        functools.partial(pack_kernel, (freq_count, blocks, chans, width, parts, tp)),
        out_shape=[unit] * freq_count,
        in_specs=[vmem],
        out_specs=[vmem] * freq_count,
        name="pack",
    )(raw)
    shared = [packed[0]] + [rotated(packed[k], "freq", k) for k in range(1, freq_count)]
    routed = pl.pallas_call(
        functools.partial(route_kernel, (pair_count, freq_count, blocks, tp, local)),
        out_shape=[jax.ShapeDtypeStruct((tp + EXTRA, LANES), jnp.float32)] * pair_count
        + [jax.ShapeDtypeStruct((REACH, tp, LANES), jnp.float32)] * pair_count,
        in_specs=[smem] + [vmem] * freq_count,
        out_specs=[vmem] * (2 * pair_count),
        scratch_shapes=[pltpu.VMEM((pair_count, tp, LANES), jnp.float32)],
        name="route",
    )(offsets, *shared)
    near = jnp.stack(
        [routed[0]] + [rotated(routed[k], "pair", k) for k in range(1, pair_count)]
    )
    far = [routed[pair_count]] + [
        rotated(routed[pair_count + k], "pair", k) for k in range(1, pair_count)
    ]
    near = [near] + [rotated(near, "freq", k) for k in range(1, freq_count)]
    near_all = list(near)
    far_all = list(far)
    for turn in range(1, sub_count):
        near_all += [rotated(value, "sub", turn) for value in near]
        far_all += [rotated(value, "sub", turn) for value in far]
    basis, lag, taper = tables(span, windows)
    cols = (REACH + 1) * width
    tiles = -(-(cols + row_count) // LANES)
    wide = -(-cols // LANES) * LANES
    rows = math.gcd(ROWS_PER_STEP, row_count)
    dims = (pair_count, freq_count, sub_count, local, seg, width, parts, tp, row_parts, windows, span)
    return pl.pallas_call(
        functools.partial(correlate_kernel, dims),
        grid=(row_count // rows,),
        out_shape=jax.ShapeDtypeStruct((1, REACH + 1, row_count, width, LAGS), jnp.bfloat16),
        in_specs=[smem] + [vmem] * (len(near_all) + len(far_all) + 3),
        out_specs=pl.BlockSpec((1, REACH + 1, rows, width, LAGS), lambda i: (0, 0, i, 0, 0)),
        scratch_shapes=[
            pltpu.SMEM((windows,), jnp.int32),
            pltpu.VMEM((tiles, windows * STEP + span, LANES), jnp.float32),
            pltpu.VMEM((windows, span, tiles * LANES), jnp.bfloat16),
            pltpu.VMEM((row_count, 2 * windows * PACK), jnp.float32),
            pltpu.VMEM((row_count, span, wide), jnp.bfloat16),
        ],
        name="correlate",
    )(pair_mask, *near_all, *far_all, basis, lag, taper)


def solution(mesh):
    return jax.shard_map(
        body,
        mesh=mesh,
        in_specs=(P("freq", ("hour", "pair", "sub")), P(("hour", "pair", "sub")), P("pair", None)),
        out_specs=P(("hour", "pair"), None, "sub", "freq", None),
        check_vma=False,
    )
```
